32 devices in a mesh: grp: 4 (over z), col: 2 (over y), lay: 4 (over x, core).
Axes of the slice: x: 2, y: 2, z: 4, core: 2. Of those that a mesh axis runs over, the one named last changes fastest.
Arguments:
- salinity: float32 [16, 128, 2048], P('lay', ('grp', 'col')), may hold values from 0.3 to 4.2
- zone_ids: int32 [16, 128, 2048], P('lay', ('grp', 'col')), may hold values from 0 to 7
- flow_speed: float32 [16, 128, 2048], P('lay', ('grp', 'col')), may hold values from 0.5 to 4
- fixed_cells: int32 [16, 128, 2048], P('lay', ('grp', 'col')), may hold values 0 or 1
- dispersivity: float32 [2, 8], replicated, may hold values from 50 to 1000
Outputs:
- salinity_next: float32 [16, 128, 2048], P('lay', 'grp', 'col')
The draws below stay inside these ranges and needn't reach their ends.
All inputs are finite; a program needn't handle non-finite values. No bound on the sum of `fixed_cells` on one device may be relied on, other than what follows from the above.
Results may differ from the reference program's by a relative error of at most 0.00005.
Values sent between devices are 32-bit elements; how exact they have to be, the bound alone decides.
No kernel may reach another device: no remote copies, remote signals or barrier semaphores. Data moves between devices by JAX's collectives and lax.ppermute only.
A program may use at most 128 MiB of HBM per device.

```python
import math
import jax
import jax.numpy as jnp
from jax import lax

NX = 2048
ZONES = 8
NZ = 16
NY = 128
N_GRP = 4


def draw_salinity(key, part):
    level_key, cell_key = jax.random.split(jax.random.fold_in(key, 17))
    bands = 2 * N_GRP
    levels = jax.random.uniform(level_key, (bands,), jnp.float32, 0.5, 3.0)
    band_of_row = jnp.arange(NY, dtype=jnp.int32) * bands // NY
    row_levels = levels[band_of_row]
    factor = jax.random.uniform(cell_key, (NZ, NY, NX), jnp.float32, 0.8, 1.2)
    return (row_levels[None, :, None] * factor).astype(jnp.float32)


def plant(entries, rng, least, top_value):
    longest = entries.shape.index(max(entries.shape))
    spots = []
    for shift in (0, 1):
        where = [jax.random.randint(jax.random.fold_in(rng, axis), (), 0, length) for axis, length in enumerate(entries.shape)]
        where[longest] = (where[longest] + shift) % entries.shape[longest]
        spots.append(tuple(where))
    return entries.at[spots[0]].set(least).at[spots[1]].set(top_value)


def level_of(rng, extent, cuts, low, largest):
    loudness = 1.0
    for axis_at, parts in cuts:
        steps = jax.random.uniform(jax.random.fold_in(jax.random.fold_in(rng, 6), axis_at), (parts,), jnp.float32, low / len(cuts), largest / len(cuts))
        loudness = loudness * jnp.repeat(jnp.exp(steps), extent[axis_at] // parts).reshape((-1,) + (1,) * (len(extent) - 1 - axis_at))
    return loudness


def setup_inputs(seed: int = 0) -> dict:
    arg_keys = jax.random.split(jax.random.key(seed), 6)
    return {
        "salinity": draw_salinity(jax.random.fold_in(arg_keys[5], 71), 0),
        "zone_ids": plant(jax.random.randint(arg_keys[1], (NZ, NY, NX), 0, ZONES), jax.random.fold_in(arg_keys[1], 1), 0, ZONES - 1).astype(jnp.int32),
        "flow_speed": jnp.clip(jnp.exp(math.log(4.0) - 2.0794415 * jax.random.uniform(arg_keys[2], (NZ, NY, NX), jnp.float32) ** level_of(arg_keys[2], (NZ, NY, NX), ((0, 4), (1, 8)), -0.2, 0.2)), 0.5, 4.0),
        "fixed_cells": plant((jax.random.randint(arg_keys[3], (NZ, NY, NX), 0, 1024) < 1).astype(jnp.int32), jax.random.fold_in(arg_keys[3], 1), 0, 1),
        "dispersivity": jnp.clip(jnp.exp(jax.random.uniform(arg_keys[4], (2, ZONES), jnp.float32, math.log(50.0), math.log(1000.0))), 50.0, 1000.0),
    }


def shifted(values, stride, line_axis, filler, heading):
    line_axis = line_axis % values.ndim
    length = values.shape[line_axis]
    edge_shape = list(values.shape)
    edge_shape[line_axis] = length
    padding = jnp.full(tuple(edge_shape), filler, values.dtype)
    padded = jnp.concatenate([padding, values, padding], axis=line_axis)
    return lax.dynamic_slice_in_dim(padded, length + heading * stride, length, axis=line_axis)


def reduce_lines(below_coef, middle, above_coef, right_side, line_axis):
    length = middle.shape[line_axis]
    levels = max(1, (length - 1).bit_length())

    def one_level(_, carry):
        below_now, middle_now, above_now, right_now, stride = carry
        weight_below = -below_now / shifted(middle_now, stride, line_axis, 1.0, -1)
        weight_above = -above_now / shifted(middle_now, stride, line_axis, 1.0, 1)
        below_next = weight_below * shifted(below_now, stride, line_axis, 0.0, -1)
        above_next = weight_above * shifted(above_now, stride, line_axis, 0.0, 1)
        middle_next = middle_now + weight_below * shifted(above_now, stride, line_axis, 0.0, -1) + weight_above * shifted(below_now, stride, line_axis, 0.0, 1)
        right_next = right_now + weight_below * shifted(right_now, stride, line_axis, 0.0, -1) + weight_above * shifted(right_now, stride, line_axis, 0.0, 1)
        return (below_next, middle_next, above_next, right_next, stride * 2)

    result = lax.fori_loop(0, levels, one_level, (below_coef, middle, above_coef, right_side, jnp.int32(1)))
    return result[3] / result[1]


def line_solve(coupling, field, line_axis):
    return reduce_lines(-coupling, 1.0 + 2.0 * coupling, -coupling, field, line_axis - field.ndim)


def couplings(zone_ids, flow_speed, fixed_cells, dispersivity):
    opened = 1.0 - fixed_cells.astype(jnp.float32)
    longit = jnp.zeros(flow_speed.shape, jnp.float32)
    transv = jnp.zeros(flow_speed.shape, jnp.float32)
    for number in range(dispersivity.shape[1]):
        matched = zone_ids == number
        longit = jnp.where(matched, dispersivity[0, number], longit)
        transv = jnp.where(matched, dispersivity[1, number], transv)
    return opened * longit * flow_speed, opened * transv * flow_speed


def reference(salinity, zone_ids, flow_speed, fixed_cells, dispersivity):
    long_coupling, trans_coupling = couplings(zone_ids, flow_speed, fixed_cells, dispersivity)
    first = line_solve(long_coupling, salinity, 2)
    second = line_solve(trans_coupling, first, 1)
    return line_solve(trans_coupling, second, 0)
```

```python
import functools

import jax
import jax.numpy as jnp
from jax import lax
from jax.experimental import pallas as pl
from jax.experimental.pallas import tpu as pltpu
from jax.sharding import PartitionSpec as P

LANES = 128
SUB = 8
F32 = jnp.float32
VMEM = pl.BlockSpec(memory_space=pltpu.VMEM)
SMEM = pl.BlockSpec(memory_space=pltpu.SMEM)
GRANT = 24 << 20


def call(body, outs, n_in, name, scratch=(), smem=(), flops=1 << 20, moved=1 << 21):
    return pl.pallas_call(
        body,
        out_shape=outs,
        in_specs=[SMEM if i in smem else VMEM for i in range(n_in)],
        out_specs=[VMEM] * len(outs),
        scratch_shapes=list(scratch),
        compiler_params=pltpu.CompilerParams(vmem_limit_bytes=GRANT),
        cost_estimate=pl.CostEstimate(flops=flops, bytes_accessed=moved, transcendentals=0),
        name=name,
    )


def shape(*dims):
    return jax.ShapeDtypeStruct(dims, F32)


def lookup(bits, values):
    level = list(values)
    for bit in bits:
        level = [jnp.where(bit, high, low) for low, high in zip(level[::2], level[1::2])]
    return level[0]


def coupling_body(n_col, tiles, zones, zone, flow, fixed, disp, longc, *parts):
    mine = lax.axis_index("col")
    depth = max(1, (zones - 1).bit_length())
    row = lambda which: [disp[which, min(i, zones - 1)] for i in range(1 << depth)]
    along, across = row(0), row(1)
    for k in range(n_col):
        first_tile = lax.rem(mine + k, n_col) * tiles
        for t in range(tiles):
            j = first_tile + t
            ids = zone[:, :, j]
            bits = [(ids & (1 << b)) != 0 for b in range(depth)]
            opened = 1.0 - fixed[:, :, j].astype(F32)
            speed = flow[:, :, j]
            longc[j] = opened * lookup(bits, along) * speed
            parts[k][t] = opened * lookup(bits, across) * speed


def shift_up(x, stride, wrap, sub, lines):
    lead = x.shape[0]
    if stride < SUB:
        later = jnp.concatenate([x[1:], pltpu.roll(x[:1], wrap, 2)], axis=0)
        return pltpu.roll(jnp.where(sub < stride, later, x), SUB - stride, 1)
    blocks = stride // SUB
    if blocks < lead:
        return jnp.concatenate([x[blocks:], pltpu.roll(x[:blocks], wrap, 2)], axis=0)
    return pltpu.roll(x, LANES - lines * (blocks // lead), 2)


def shift_down(x, stride, wrap, sub, lines):
    lead = x.shape[0]
    if stride < SUB:
        earlier = jnp.concatenate([pltpu.roll(x[-1:], LANES - wrap, 2), x[:-1]], axis=0)
        return pltpu.roll(jnp.where(sub >= SUB - stride, earlier, x), stride, 1)
    blocks = stride // SUB
    if blocks < lead:
        return jnp.concatenate([pltpu.roll(x[-blocks:], LANES - wrap, 2), x[:-blocks]], axis=0)
    return pltpu.roll(x, lines * (blocks // lead), 2)


def column_body(n_col, tiles, sal, longc, *rest):
    outs, (tc, td, g_s, l_s, d_s, xs) = rest[:n_col], rest[n_col:]
    n_j = longc.shape[0]
    lines = longc.shape[1] * longc.shape[2] * SUB
    halves = LANES // lines
    blocks = n_j // halves
    step = LANES // SUB
    for b in range(blocks):
        block = jnp.concatenate(
            [longc[h * blocks + b].reshape(lines, LANES) for h in range(halves)], axis=0
        )
        tc[b] = block.T
        block = jnp.concatenate(
            [sal[:, :, h * blocks + b].reshape(lines, LANES) for h in range(halves)], axis=0
        )
        td[b] = block.T

    full = (blocks, SUB, LANES)
    sub = lax.broadcasted_iota(jnp.int32, full, 1)
    lane = lax.broadcasted_iota(jnp.int32, full, 2)
    lead = lax.broadcasted_iota(jnp.int32, full, 0)
    begins = (sub == 0) & (lead == 0) & (lane < lines)
    ends = (sub == SUB - 1) & (lead == blocks - 1) & (lane >= LANES - lines)

    at = lambda ref, q: ref[:, pl.ds(q, SUB, stride=step), :]
    g = low = d = None
    for q in range(step - 1):
        s = at(tc, q)
        r = at(td, q)
        if q == 0:
            inv = 1.0 / (1.0 + 2.0 * s)
            g = s * inv
            low = jnp.where(begins, 0.0, g)
            d = r * inv
        else:
            inv = 1.0 / ((1.0 + 2.0 * s) - s * g)
            g = s * inv
            low = g * low
            d = r * inv + g * d
        g_s[q] = g
        l_s[q] = low
        d_s[q] = d
    f_d, f_l, f_u = d, low, g
    for q in range(step - 3, -1, -1) if step > 2 else ():
        gq = g_s[q]
        f_d = d_s[q] + gq * f_d
        f_l = l_s[q] + gq * f_l
        f_u = gq * f_u
    up = functools.partial(shift_up, wrap=LANES - lines, sub=sub, lines=lines)
    down = functools.partial(shift_down, wrap=LANES - lines, sub=sub, lines=lines)
    n_d = jnp.where(ends, 0.0, up(f_d, 1))
    n_l = jnp.where(ends, 0.0, up(f_l, 1))
    n_u = jnp.where(ends, 0.0, up(f_u, 1))
    s = at(tc, step - 1)
    r = at(td, step - 1)
    inv = 1.0 / ((1.0 + 2.0 * s) - s * g - s * n_l)
    si = s * inv
    a = si * low
    c = si * n_u
    x = r * inv + si * (d + n_d)
    stride = 1
    total = n_j * SUB
    while stride < total:
        a_d, a_u = down(a, stride), up(a, stride)
        c_d, c_u = down(c, stride), up(c, stride)
        x_d, x_u = down(x, stride), up(x, stride)
        inv = 1.0 / (1.0 - a * c_d - c * a_u)
        x = (x + a * x_d + c * x_u) * inv
        a = a * a_d * inv
        c = c * c_u * inv
        stride *= 2
    before = down(x, 1)
    td[:, pl.ds(step - 1, SUB, stride=step), :] = x
    for q in range(step - 2, -1, -1):
        x = d_s[q] + l_s[q] * before + g_s[q] * x
        td[:, pl.ds(q, SUB, stride=step), :] = x
    for b in range(blocks):
        block = td[b].T
        for h in range(halves):
            xs[h * blocks + b] = block[h * lines : (h + 1) * lines].reshape(xs.shape[1:])
    mine = lax.axis_index("col")
    for k in range(n_col):
        outs[k][...] = xs[pl.ds(lax.rem(mine + k, n_col) * tiles, tiles)]


def row_tile(ref, layer, row):
    return ref[:, layer * row[1] + row[0], :]


def rows_in_order(parts, held, n_col):
    mine = lax.axis_index("col")
    for k, part in enumerate(parts):
        held[lax.rem(mine + n_col - k, n_col)] = part[...].reshape(held.shape[1:])


def row_factor_body(n_col, layers, rows, *refs):
    parts = refs[:n_col]
    t_out, h_out, g_out, l_out, u_out, edges, held = refs[n_col:]
    tiles = held.shape[1] // (layers * rows)
    rows_in_order(parts, held, n_col)

    def load(source, row):
        return jnp.stack(
            [
                held[source, pl.ds(layer * rows + row, tiles, stride=layers * rows), :]
                for layer in range(layers)
            ]
        )

    def forward(source, carry):
        g, low = carry
        for row in range(rows):
            s = load(source, row)
            inv = 1.0 / ((1.0 + 2.0 * s) - s * g)
            g = s * inv
            low = g * low
            at = source * rows + row
            t_out[at] = s
            h_out[at] = inv
            g_out[at] = g
            l_out[at] = low
        return g, low

    zero = jnp.zeros((layers, tiles, LANES), F32)
    g, low = lax.fori_loop(0, n_col, forward, (zero, zero + 1.0), unroll=n_col <= 2)
    total = n_col * rows
    u_out[total - 1] = g
    edges[2] = low
    edges[3] = g

    def backward(turn, carry):
        low, high = carry
        source = n_col - 1 - turn
        for row in range(rows - 1, -1, -1):
            at = source * rows + row
            gq = g_out[at]
            low = l_out[at] + gq * low
            high = gq * high
            l_out[at] = low
            u_out[at] = high
        return low, high

    low, high = lax.fori_loop(0, n_col, backward, (zero, zero + 1.0), unroll=n_col <= 2)
    edges[0] = low
    edges[1] = high


def row_sweep_body(n_col, layers, rows, *refs):
    parts = refs[:n_col]
    h, g, d_out, edges, held = refs[n_col:]
    tiles = held.shape[1] // (layers * rows)
    rows_in_order(parts, held, n_col)

    def forward(source, d):
        for row in range(rows):
            r = jnp.stack(
                [
                    held[source, pl.ds(layer * rows + row, tiles, stride=layers * rows), :]
                    for layer in range(layers)
                ]
            )
            at = source * rows + row
            d = r * h[at] + g[at] * d
            d_out[at] = d
        return d

    zero = jnp.zeros((layers, tiles, LANES), F32)
    d = lax.fori_loop(0, n_col, forward, zero, unroll=n_col <= 2)
    edges[1] = d

    def backward(turn, d):
        source = n_col - 1 - turn
        for row in range(rows - 1, -1, -1):
            at = source * rows + row
            d = d_out[at] + g[at] * d
            d_out[at] = d
        return d

    d = lax.fori_loop(0, n_col, backward, zero, unroll=n_col <= 2)
    edges[0] = d


def row_join_body(n_grp, *refs):
    coefs, fields = refs[:n_grp], refs[n_grp : 2 * n_grp]
    d_in, l_in, u_in, out, co, fi, firsts, lasts = refs[2 * n_grp :]
    mine = lax.axis_index("grp")
    for k in range(n_grp):
        block = lax.rem(mine + n_grp - k, n_grp)
        co[block] = coefs[k][...]
        fi[block] = fields[k][...]
    zero = jnp.zeros(fi.shape[2:], F32)
    p, q = zero, zero
    steps = []
    for b in range(n_grp):
        f_l, f_u, l_l, l_u = (co[b, i] for i in range(4))
        inv = 1.0 / (1.0 - f_l * q)
        start = (fi[b, 0] + f_l * p) * inv
        ratio = f_u * inv
        link = l_l * q
        p = fi[b, 1] + l_l * p + link * start
        q = l_u + link * ratio
        steps.append((start, ratio, p, q))
    after = zero
    firsts[n_grp] = zero
    lasts[0] = zero
    for b in range(n_grp - 1, -1, -1):
        start, ratio, p, q = steps[b]
        lasts[b + 1] = p + q * after
        after = start + ratio * after
        firsts[b] = after
    before, after = lasts[mine], firsts[mine + 1]

    total, unit = d_in.shape[0], 8

    def one(i, _):
        at = pl.ds(i * unit, unit)
        out[at] = d_in[at] + l_in[at] * before + u_in[at] * after
        return 0

    lax.fori_loop(0, total // unit, one, 0, unroll=total // unit <= 4)


def layer_order(m, half, layers, total):
    along = jnp.where(half == 0, m, total - 1 - m)
    return along // layers, lax.rem(along, layers)


def own_and_half(n_lay):
    mine = lax.axis_index("lay")
    n_half = max(n_lay // 2, 1)
    return lax.rem(mine, n_half), mine // n_half, n_half


def gather_half(parts, held, n_lay):
    place, half, n_half = own_and_half(n_lay)
    for k, part in enumerate(parts):
        held[lax.rem(place + n_half - k, n_half)] = part[...]
    return place, half, n_half


UNIT = 8


def layer_factor_body(n_lay, *refs):
    n_half = max(n_lay // 2, 1)
    parts = refs[:n_half]
    h_out, g_out, last, held = refs[n_half:]
    place, half, n_half = gather_half(parts, held, n_lay)
    layers, rows = held.shape[2], held.shape[1]
    total = n_half * layers

    def one(i, _):
        at = pl.ds(i * UNIT, UNIT)
        g = None
        for m in range(total):
            device, layer = layer_order(m, half, layers, total)
            s = held[device, at, layer]
            pivot = 1.0 + 2.0 * s
            if m:
                pivot = pivot - s * g
            inv = 1.0 / pivot
            g = s * inv
            h_out[m, at] = inv
            g_out[m, at] = g
        last[at] = g
        return 0

    lax.fori_loop(0, rows // UNIT, one, 0)


def layer_sweep_body(n_lay, *refs):
    n_half = max(n_lay // 2, 1)
    parts = refs[:n_half]
    h, g, d_out, last, held = refs[n_half:]
    place, half, n_half = gather_half(parts, held, n_lay)
    layers, rows = held.shape[2], held.shape[1]
    total = n_half * layers

    def one(i, _):
        at = pl.ds(i * UNIT, UNIT)
        d = None
        for m in range(total):
            device, layer = layer_order(m, half, layers, total)
            r = held[device, at, layer] * h[m, at]
            d = r if m == 0 else r + g[m, at] * d
            d_out[m, at] = d
        last[at] = d
        return 0

    lax.fori_loop(0, rows // UNIT, one, 0)


def layer_join_body(n_lay, other_d, other_g, d_in, g_in, out, solved):
    place, half, n_half = own_and_half(n_lay)
    total, rows, tiles = d_in.shape[0], d_in.shape[1], d_in.shape[2]
    layers = total // n_half
    groups = rows // SUB

    def one(i, _):
        at = pl.ds(i * UNIT, UNIT)
        g = g_in[total - 1, at]
        x = (d_in[total - 1, at] + g * other_d[at]) / (1.0 - g * other_g[at])
        solved[total - 1] = x
        for m in range(total - 2, -1, -1):
            x = d_in[m, at] + g_in[m, at] * x
            solved[m] = x
        for layer in range(layers):
            along = place * layers + layer
            m = jnp.where(half == 0, along, total - 1 - along)
            values = solved[m]
            for r in range(SUB):
                start = (layer * groups + i) * tiles * SUB + r
                out[pl.ds(start, tiles, stride=SUB), :] = values[r]
        return 0

    lax.fori_loop(0, groups, one, 0)


def solution(mesh):
    n_grp, n_col, n_lay = (mesh.shape[a] for a in ("grp", "col", "lay"))
    n_half = max(n_lay // 2, 1)

    def hop(value, axis, size, k):
        return lax.ppermute(value, axis, [(i, (i + k) % size) for i in range(size)])

    def hop_half(value, k):
        pairs = [
            (h * n_half + i, h * n_half + (i + k) % n_half)
            for h in range(n_lay // n_half)
            for i in range(n_half)
        ]
        return lax.ppermute(value, "lay", pairs)

    def across(value):
        return lax.ppermute(value, "lay", [(i, n_lay - 1 - i) for i in range(n_lay)])

    def per_device(salinity, zone_ids, flow_speed, fixed_cells, dispersivity):
        layers, rows, length = salinity.shape
        n_j = length // LANES
        tiles = n_j // n_col
        groups = rows // SUB
        total = rows * n_col

        def tiled(x):
            return x.reshape(layers, groups, SUB, n_j, LANES).transpose(0, 1, 3, 2, 4)

        part = shape(tiles, layers, groups, SUB, LANES)
        whole = shape(n_j, layers, groups, SUB, LANES)
        zones = dispersivity.shape[1]
        longc, *t_parts = call(
            functools.partial(coupling_body, n_col, tiles, zones),
            [whole] + [part] * n_col,
            4,
            "couplings",
            smem=(3,),
        )(tiled(zone_ids), tiled(flow_speed), tiled(fixed_cells), dispersivity)
        t_parts = [t_parts[0]] + [hop(t_parts[k], "col", n_col, k) for k in range(1, n_col)]

        lines = layers * rows
        blocks = n_j * lines // LANES
        step = LANES // SUB
        square = pltpu.VMEM((blocks, LANES, LANES), F32)
        chain = pltpu.VMEM((step - 1, blocks, SUB, LANES), F32)
        parts = call(
            functools.partial(column_body, n_col, tiles),
            [part] * n_col,
            2,
            "columns",
            [square, square, chain, chain, chain, pltpu.VMEM(whole.shape, F32)],
        )(tiled(salinity), longc)
        parts = [parts[0]] + [hop(parts[k], "col", n_col, k) for k in range(1, n_col)]

        line = (layers, tiles, LANES)
        held = pltpu.VMEM((n_col, tiles * layers * rows, LANES), F32)
        field = shape(total, *line)
        t, h, g, low, high, coefs = call(
            functools.partial(row_factor_body, n_col, layers, rows),
            [field] * 5 + [shape(4, *line)],
            n_col,
            "row_factor",
            [held],
        )(*t_parts)
        coefs = [coefs] + [hop(coefs, "grp", n_grp, k) for k in range(1, n_grp)]
        t_half = [t] + [hop_half(t, k) for k in range(1, n_half)]
        stacked = shape(n_half * layers, total, tiles, LANES)
        plane = shape(total, tiles, LANES)
        held_half = pltpu.VMEM((n_half, total, *line), F32)
        lh, lg, ratio = call(
            functools.partial(layer_factor_body, n_lay),
            [stacked, stacked, plane],
            n_half,
            "layer_factor",
            [held_half],
        )(*t_half)
        other_ratio = across(ratio)

        d, edges = call(
            functools.partial(row_sweep_body, n_col, layers, rows),
            [field, shape(2, *line)],
            n_col + 2,
            "row_sweep",
            [held],
        )(*parts, h, g)
        edges = [edges] + [hop(edges, "grp", n_grp, k) for k in range(1, n_grp)]
        (second,) = call(
            functools.partial(row_join_body, n_grp),
            [field],
            2 * n_grp + 3,
            "row_join",
            [
                pltpu.VMEM((n_grp, 4, *line), F32),
                pltpu.VMEM((n_grp, 2, *line), F32),
                pltpu.VMEM((n_grp + 1, *line), F32),
                pltpu.VMEM((n_grp + 1, *line), F32),
            ],
        )(*coefs, *edges, d, low, high)

        halves = [second] + [hop_half(second, k) for k in range(1, n_half)]
        ld, last = call(
            functools.partial(layer_sweep_body, n_lay),
            [stacked, plane],
            n_half + 2,
            "layer_sweep",
            [held_half],
        )(*halves, lh, lg)
        (out,) = call(
            functools.partial(layer_join_body, n_lay),
            [shape(layers * total * tiles, LANES)],
            4,
            "layer_join",
            [pltpu.VMEM((n_half * layers, UNIT, tiles, LANES), F32)],
        )(across(last), other_ratio, ld, lg)
        out = out.reshape(layers, total // SUB, tiles, SUB, LANES).transpose(0, 1, 3, 2, 4)
        return out.reshape(layers, total, tiles * LANES)

    placed = (P("lay", ("grp", "col"), None),) * 4 + (P(),)
    return jax.shard_map(
        per_device, mesh=mesh, in_specs=placed, out_specs=P("lay", "grp", "col"), check_vma=False
    )
```
